256 devices in a mesh: kmer: 32 (over z, y), samp: 8 (over x, core).
Axes of the slice: x: 4, y: 4, z: 8, core: 2. Of those that a mesh axis runs over, the one named last changes fastest.
Arguments:
- abundance: float32 [65536, 8192], P('kmer', 'samp'), may hold values from 1 to 100
- loadings: float32 [65536, 256], P('kmer', 'samp'), may hold values from 0.01 to 5, as said below
- activity: float32 [256, 8192], P('kmer', 'samp'), may hold values from 0.01 to 5, as said below
Outputs:
- new_loadings: float32 [65536, 256], P('kmer', 'samp')
- new_activity: float32 [256, 8192], P('kmer', 'samp')
The draws below stay inside these ranges and needn't reach their ends.
Inputs may be any that keep to these rules, and one draw needn't show every extreme that they name: `loadings`: positive entries. `activity`: positive entries.
All inputs are finite; a program needn't handle non-finite values.
Results may differ from the reference program's by a relative error of at most 0.0001.
Values sent between devices are 32-bit elements; how exact they have to be, the bound alone decides.
No kernel may reach another device: no remote copies, remote signals or barrier semaphores. Data moves between devices by JAX's collectives and lax.ppermute only.
A program may use at most 64 MiB of HBM per device.

```python
import math
import jax
import jax.numpy as jnp
from jax import lax

K = 256
MD = 2048
M = 65536
N = 8192
N_KMER = 32


def draw_loadings(key, part):
    first = jax.random.fold_in(jax.random.fold_in(key, 11), 0)
    rising = 1.0 + 2.0 * jnp.arange(M, dtype=jnp.float32)[:, None] / (M - 1)
    base = jnp.exp(jax.random.uniform(first, (M, K), jnp.float32, jnp.log(0.05), jnp.log(0.5)))
    return base * rising


def draw_activity(key, part):
    first = jax.random.fold_in(jax.random.fold_in(key, 23), 0)
    third = jax.random.fold_in(jax.random.fold_in(key, 23), 2)
    position = jnp.arange(N, dtype=jnp.float32)[None, :] / (N - 1)
    rising = 1.0 + 2.0 * position
    slopes = jax.random.uniform(third, (K, 1), jnp.float32, -1.0, 1.0)
    profile = jnp.exp(slopes * (2.0 * position - 1.0))
    base = jnp.exp(jax.random.uniform(first, (K, N), jnp.float32, jnp.log(0.05), jnp.log(0.5)))
    return base * rising * profile


def steps_of(stream_key, extent, cuts, smallest, high):
    loudness, own = 1.0, jax.random.fold_in(stream_key, 6)
    for axis_at, shards_of in cuts:
        draws = jnp.exp(jax.random.uniform(jax.random.fold_in(own, axis_at), (shards_of,), jnp.float32, smallest / len(cuts), high / len(cuts)))
        loudness = loudness * jnp.repeat(draws, extent[axis_at] // shards_of).reshape([-1 if axis == axis_at else 1 for axis in range(len(extent))])
    return loudness


def setup_inputs(seed: int = 0) -> dict:
    key_of = jax.random.split(jax.random.key(seed), 4)
    abundance = jnp.clip(jnp.exp(math.log(100.0) - 4.6051702 * jax.random.uniform(key_of[0], (M, N), jnp.float32) ** steps_of(key_of[0], (M, N), ((0, 32), (1, 8)), -0.2, 0.2)), 1.0, 100.0)
    loadings = draw_loadings(jax.random.fold_in(key_of[3], 71), 0)
    activity = draw_activity(jax.random.fold_in(key_of[3], 71), 0)
    return {"abundance": abundance, "loadings": loadings, "activity": activity}


def reference(abundance, loadings, activity):
    highest = lax.Precision.HIGHEST
    activity_sums = jnp.sum(activity, axis=1)
    data_blocks = abundance.reshape(N_KMER, MD, N)
    load_blocks = loadings.reshape(N_KMER, MD, K)

    def update_rows(block_pair):
        data_block, load_block = block_pair
        rebuilt = jnp.dot(load_block, activity, precision=highest, preferred_element_type=jnp.float32)
        quotient = data_block / rebuilt
        numer = jnp.dot(quotient, activity.T, precision=highest, preferred_element_type=jnp.float32)
        return load_block * numer / activity_sums

    new_blocks = lax.map(update_rows, (data_blocks, load_blocks))
    new_loadings = new_blocks.reshape(N_KMER * MD, K)
    loading_sums = jnp.sum(new_loadings, axis=0)

    def accumulate(total, block_pair):
        data_block, load_block = block_pair
        rebuilt = jnp.dot(load_block, activity, precision=highest, preferred_element_type=jnp.float32)
        quotient = data_block / rebuilt
        return total + jnp.dot(load_block.T, quotient, precision=highest, preferred_element_type=jnp.float32), None

    numer_h, _ = lax.scan(accumulate, jnp.zeros((K, N), jnp.float32), (data_blocks, new_blocks))
    new_activity = activity * numer_h / loading_sums[:, None]
    return new_loadings, new_activity
```

```python
import functools

import jax
import jax.numpy as jnp
from jax import lax
from jax.experimental import pallas as pl
from jax.experimental.pallas import tpu as pltpu
from jax.sharding import PartitionSpec as P

NZ, NY, NX, NC = 8, 4, 4, 2
BOTH = ("kmer", "samp")
Z_ORDER = (0, 4, 2, 6, 1, 5, 3, 7)
TILE = 512
LANES = 128


def pairs_of(move):
    out = []
    for z in range(NZ):
        for y in range(NY):
            for x in range(NX):
                for c in range(NC):
                    tz, ty, tx, tc = move(z, y, x, c, 1 - 2 * c)
                    source = ((z * NY + y) * NX + x) * NC + c
                    target = (((tz % NZ) * NY + ty % NY) * NX + tx % NX) * NC + tc
                    out.append((source, target))
    return out


def shift(array, dz=0, dy=0, dx=0):
    return lax.ppermute(
        array, BOTH, pairs_of(lambda z, y, x, c, d: (z + d * dz, y + d * dy, x + d * dx, c))
    )


def swap_cores(array):
    return lax.ppermute(array, BOTH, pairs_of(lambda z, y, x, c, d: (z, y, x, 1 - c)))


def gather_ring4(block, **step):
    back = {axis: -by for axis, by in step.items()}
    third = shift(block, **step)
    first = shift(block, **back)
    second = shift(third, **step)
    return block, first, second, third


def gather_z(block):
    for by in (4, 2, 1):
        block = jnp.concatenate([block, shift(block, dz=by)], axis=0)
    return block


def scatter_ring4(parts, **step):
    back = {axis: -by for axis, by in step.items()}
    relay = shift(parts[2], **step)
    down = shift(parts[3], **back)
    up = shift(parts[1] + relay, **step)
    return parts[0] + down + up


def scatter_z(part):
    for by in (1, 2, 4):
        half = part.shape[0] // 2
        part = part[:half] + shift(part[half:], dz=by)
    return part


def split(value):
    high = value.astype(jnp.bfloat16)
    low = (value - high.astype(jnp.float32)).astype(jnp.bfloat16)
    return high, low


def dot3(left, right, dims):
    dot = functools.partial(
        lax.dot_general, dimension_numbers=(dims, ((), ())), preferred_element_type=jnp.float32
    )
    return dot(left[0], right[0]) + (dot(left[0], right[1]) + dot(left[1], right[0]))


def place_of(where, z_block):
    x, c, d = where[2], where[3], where[4]
    own = (z_block & 1) == c
    steps = (((z_block >> 1) - x) * jnp.where(own, d, -d)) & (NX - 1)
    return jnp.where(own, 0, NX) + steps


def blocks_of(where, sign):
    z, y, d = where[0], where[1], where[4]
    for t in range(NY):
        for at, by in enumerate(Z_ORDER):
            z_block = (z + sign * d * by) & (NZ - 1)
            y_block = (y + d * t) & (NY - 1)
            row = place_of(where, z_block) * 32 + y_block * 8
            yield t, at * 8, pl.multiple_of(row, 8)


def rows_kernel(where, w_own, w_other, h0, h1, h2, h3, a, k0, k1, k2, k3, send, hh, hl, held):
    step = pl.program_id(0)
    width = a.shape[0]

    @pl.when(step == 0)
    def _():
        pieces = (h0, h1, h2, h3)
        for t, at, row in blocks_of(where, -1):
            held[pl.ds(row, 8), :] = pieces[t][at : at + 8, :]
        high, low = split(held[...])
        hh[...] = high
        hl[...] = low
        total = jnp.sum(held[...], axis=1, keepdims=True)
        total = jnp.broadcast_to(total, (total.shape[0], LANES))
        last = k0.shape[1] - LANES
        for t, out in enumerate((k0, k1, k2, k3)):
            out[:, last:] = total[32 * t : 32 * t + 32]
        send[:, last:] = total[128:]

    h = (hh[...], hl[...])
    w = split(jnp.concatenate([w_own[...], w_other[...]], axis=0))
    rebuilt = dot3(w, h, ((0,), (0,)))
    quotient = split(a[...] / rebuilt)
    numer = dot3(h, quotient, ((1,), (1,)))
    columns = pl.ds(pl.multiple_of(step * width, width), width)
    for t, out in enumerate((k0, k1, k2, k3)):
        out[:, columns] = numer[32 * t : 32 * t + 32]
    send[:, columns] = numer[128:]


def columns_kernel(where, w_own, w_other, hh, hl, a, p0, p1, p2, p3, total):
    step = pl.program_id(0)
    samples = a.shape[1]
    h = (hh[...], hl[...])
    whole = jnp.concatenate([w_own[...], w_other[...]], axis=0)
    w = split(whole)
    rebuilt = dot3(w, h, ((0,), (0,)))
    quotient = split(a[...] / rebuilt)
    numer = dot3(w, quotient, ((1,), (0,)))
    sums = jnp.broadcast_to(jnp.sum(whole, axis=1, keepdims=True), (whole.shape[0], LANES))

    @pl.when(step == 0)
    def _():
        total[:, :samples] = numer
        total[:, samples:] = sums

    @pl.when(step > 0)
    def _():
        total[:, :samples] += numer
        total[:, samples:] += sums

    @pl.when(step == pl.num_programs(0) - 1)
    def _():
        outs = (p0, p1, p2, p3)
        for t, at, row in blocks_of(where, 1):
            outs[t][at : at + 8, :] = total[pl.ds(row, 8), :]


def whole_spec(shape):
    return pl.BlockSpec(shape, lambda i, where: (0, 0))


def call_kernel(body, where, ins, specs, outs, scratch, steps, flops, moved):
    return pl.pallas_call(
        body,
        grid_spec=pltpu.PrefetchScalarGridSpec(
            num_scalar_prefetch=1,
            grid=(steps,),
            in_specs=specs,
            out_specs=[whole_spec(o.shape) for o in outs],
            scratch_shapes=scratch,
        ),
        out_shape=outs,
        cost_estimate=pl.CostEstimate(flops=flops, bytes_accessed=moved, transcendentals=0),
        compiler_params=pltpu.CompilerParams(dimension_semantics=("arbitrary",), vmem_limit_bytes=40 << 20),
    )(where, *ins)


def per_device(abundance, loadings, activity):
    f32 = jnp.float32
    rows, samples = abundance.shape
    own_rank, own_rows = loadings.shape[1], activity.shape[0]
    rank = own_rank * NX * NC
    half = rank // 2
    kmer, samp = lax.axis_index("kmer"), lax.axis_index("samp")
    c = samp & 1
    where = jnp.stack([kmer >> 2, kmer & 3, samp >> 1, c, 1 - 2 * c]).astype(jnp.int32)
    steps = rows // TILE
    flops = 4 * 3 * rows * samples * rank
    moved = rows * samples * 4

    w_spec = pl.BlockSpec((half, TILE), lambda i, where: (0, i))
    a_spec = pl.BlockSpec((TILE, samples), lambda i, where: (i, 0))

    w_mine = loadings.T
    h_parts = gather_ring4(gather_z(activity), dy=1)
    w_own = jnp.concatenate(gather_ring4(w_mine, dx=1), axis=0)
    w_other = swap_cores(w_own)

    shape = jax.ShapeDtypeStruct
    *keep, send, hh, hl = call_kernel(
        rows_kernel,
        where,
        (w_own, w_other, *h_parts, abundance),
        [w_spec, w_spec] + [whole_spec(h.shape) for h in h_parts] + [a_spec],
        [shape((own_rank, rows + LANES), f32)] * 4
        + [shape((half, rows + LANES), f32)]
        + [shape((rank, samples), jnp.bfloat16)] * 2,
        [pltpu.VMEM((rank, samples), f32)],
        steps,
        flops,
        moved,
    )
    got = swap_cores(send)
    parts = [k + got[own_rank * t : own_rank * (t + 1)] for t, k in enumerate(keep)]
    numer_w = scatter_ring4(parts, dx=1)
    w_new = w_mine * numer_w[:, :rows] / numer_w[:, rows : rows + 1]

    n_own = jnp.concatenate(gather_ring4(w_new, dx=1), axis=0)
    n_other = swap_cores(n_own)
    parts = call_kernel(
        columns_kernel,
        where,
        (n_own, n_other, hh, hl, abundance),
        [w_spec, w_spec, whole_spec(hh.shape), whole_spec(hl.shape), a_spec],
        [shape((own_rows * NZ, samples + LANES), f32)] * 4,
        [pltpu.VMEM((rank, samples + LANES), f32)],
        steps,
        flops,
        moved,
    )
    numer_h = scatter_z(scatter_ring4(parts, dy=1))
    new_activity = activity * numer_h[:, :samples] / numer_h[:, samples : samples + 1]
    return (w_new.T, new_activity)


def solution(mesh):
    in_specs = (P("kmer", "samp"), P("kmer", "samp"), P("kmer", "samp"))
    out_specs = (P("kmer", "samp"), P("kmer", "samp"))
    return jax.shard_map(
        per_device, mesh=mesh, in_specs=in_specs, out_specs=out_specs, check_vma=False
    )
```

```python
import functools

import jax
import jax.numpy as jnp
from jax import lax
from jax.experimental import pallas as pl
from jax.experimental.pallas import tpu as pltpu
from jax.sharding import PartitionSpec as P


NZ, NY, NX, NC = 8, 4, 4, 2
BOTH = ("kmer", "samp")
Z_GROUPS = [[z * NY + y for z in range(NZ)] for y in range(NY)]
Z_ORDER = (0, 4, 1, 5, 7, 3, 2, 6)
TILE = 512
CHUNKS = 2
SPLIT = 1
LANES = 128


def pairs_of(move):
    out = []
    for z in range(NZ):
        for y in range(NY):
            for x in range(NX):
                for c in range(NC):
                    tz, ty, tx, tc = move(z, y, x, c, 1 - 2 * c)
                    source = ((z * NY + y) * NX + x) * NC + c
                    target = (((tz % NZ) * NY + ty % NY) * NX + tx % NX) * NC + tc
                    out.append((source, target))
    return out


def shift(array, dz=0, dy=0, dx=0):
    pairs = pairs_of(lambda z, y, x, c, d: (z + d * dz, y + d * dy, x + d * dx, c))
    return lax.ppermute(array, BOTH, pairs)


def swap_cores(array):
    pairs = pairs_of(lambda z, y, x, c, d: (z, y, x, 1 - c))
    return lax.ppermute(array, BOTH, pairs)


RING = (2, 1, -1)


def gather_ring4(block, axis):
    second, third, first = (shift(block, **{axis: by}) for by in RING)
    return block, first, second, third


def gather_z(block):
    block = jnp.concatenate([block, shift(block, dz=4)], axis=0)
    moved = [shift(block, dz=by) for by in (1, -1, 2)]
    return jnp.concatenate([block, *moved], axis=0)


def scatter_ring4(parts, axis):
    got = [shift(parts[by % 4], **{axis: by}) for by in RING]
    return (parts[0] + got[0]) + (got[1] + got[2])


def scatter_z(part):
    blocks = part.reshape(NZ, part.shape[0] // NZ, part.shape[1])
    return jnp.sum(lax.all_to_all(blocks, "kmer", 0, 0, axis_index_groups=Z_GROUPS), axis=0)


def split(value):
    high = value.astype(jnp.bfloat16)
    low = (value - high.astype(jnp.float32)).astype(jnp.bfloat16)
    return high, low


def dot3(left, right, dims):
    dot = functools.partial(
        lax.dot_general, dimension_numbers=(dims, ((), ())), preferred_element_type=jnp.float32
    )
    return dot(left[0], right[0]) + (dot(left[0], right[1]) + dot(left[1], right[0]))


def place_of(where, z_block):
    x, c, d = where[2], where[3], where[4]
    own = (z_block & 1) == c
    steps = (((z_block >> 1) - x) * jnp.where(own, d, -d)) & (NX - 1)
    return jnp.where(own, 0, NX) + steps


def blocks_of(where, gathered):
    z, y, d = where[0], where[1], where[4]
    for at, by in enumerate(Z_ORDER):
        z_block = (z - d * by) & (NZ - 1) if gathered else at
        place = place_of(where, z_block) * 32
        for t in range(NY):
            row = place + ((y + d * t) & (NY - 1)) * 8
            yield t, at * 8, pl.multiple_of(row, 8)


def copy_of(i, a, held, sems, row, column):
    at = pl.multiple_of(i * TILE, TILE)
    source = a.at[pl.ds(row + at, TILE), pl.ds(column, held.shape[1])]
    return pltpu.make_async_copy(source, held.at[pl.ds(at, TILE), :], sems.at[i])


def start_copies(*block):
    for i in range(block[1].shape[0] // TILE):
        copy_of(i, *block).start()


def rows_body(row, w_own, w_other, hh, hl, a, outs, held, sems, prepare=None):
    block = (a, held, sems, row, 0)
    start_copies(*block)
    if prepare is not None:
        prepare()

    def tile(i, _):
        at = pl.multiple_of(i * TILE, TILE)
        columns = pl.ds(row + at, TILE)
        h = (hh[...], hl[...])
        w = split(jnp.concatenate([w_own[:, columns], w_other[:, columns]], axis=0))
        rebuilt = dot3(w, h, ((0,), (0,)))
        copy_of(i, *block).wait()
        quotient = split(held[pl.ds(at, TILE), :] / rebuilt)
        numer = dot3(h, quotient, ((1,), (1,)))
        columns = pl.ds(at, TILE)
        for t, out in enumerate(outs[:-1]):
            out[:, columns] = numer[32 * t : 32 * t + 32]
        outs[-1][:, columns] = numer[128:]
        return 0

    lax.fori_loop(0, held.shape[0] // TILE, tile, 0)


def first_rows_kernel(
    where, w_own, w_other, h0, h1, h2, h3, a, k0, k1, k2, k3, send, hh, hl, held, sems, h_all
):
    outs = (k0, k1, k2, k3, send)
    pieces = (h0, h1, h2, h3)

    def prepare():
        for t, at, row in blocks_of(where, True):
            h_all[pl.ds(row, 8), :] = pieces[t][at : at + 8, :]
        high, low = split(h_all[...])
        hh[...] = high
        hl[...] = low
        total = jnp.sum(h_all[...], axis=1, keepdims=True)
        total = jnp.broadcast_to(total, (total.shape[0], LANES))
        last = k0.shape[1] - LANES
        for t, out in enumerate(outs[:-1]):
            out[:, last:] = total[32 * t : 32 * t + 32]
        send[:, last:] = total[128:]

    rows_body(0, w_own, w_other, hh, hl, a, outs, held, sems, prepare)


def rows_kernel(row, where, w_own, w_other, hh, hl, a, k0, k1, k2, k3, send, held, sems):
    rows_body(row, w_own, w_other, hh, hl, a, (k0, k1, k2, k3, send), held, sems)


def columns_body(row, column, w_own, w_other, hh, hl, a, total, held, sems):
    block = (a, held, sems, row, column)
    samples = held.shape[1]
    start_copies(*block)

    def tile(i, _):
        at = pl.multiple_of(i * TILE, TILE)
        columns = slice(column, column + samples)
        h = (hh[:, columns], hl[:, columns])
        w = split(jnp.concatenate([w_own[:, pl.ds(at, TILE)], w_other[:, pl.ds(at, TILE)]], axis=0))
        rebuilt = dot3(w, h, ((0,), (0,)))
        copy_of(i, *block).wait()
        quotient = split(held[pl.ds(at, TILE), :] / rebuilt)
        total[:, :samples] += dot3(w, quotient, ((1,), (0,)))
        return 0

    lax.fori_loop(0, held.shape[0] // TILE, tile, 0)


def sums_of(w_own, w_other):
    whole = jnp.concatenate([w_own[...], w_other[...]], axis=0)
    total = jnp.sum(whole, axis=1, keepdims=True)
    return jnp.broadcast_to(total, (total.shape[0], LANES))


def columns_kernel(where, w_own, w_other, hh, hl, a, total, held, sems):
    samples = held.shape[1]
    total[:, :samples] = jnp.zeros((total.shape[0], samples), jnp.float32)
    total[:, samples:] = sums_of(w_own, w_other)
    columns_body(0, 0, w_own, w_other, hh, hl, a, total, held, sems)


def last_columns_kernel(
    row, column, where, w_own, w_other, hh, hl, a, start, p0, p1, p2, p3, held, sems, total
):
    samples = held.shape[1]
    total[:, :samples] = start[:, column : column + samples]
    if p0.shape[1] > samples:
        total[:, samples:] = start[:, start.shape[1] - LANES :] + sums_of(w_own, w_other)
    columns_body(row, column, w_own, w_other, hh, hl, a, total, held, sems)
    outs = (p0, p1, p2, p3)
    for t, at, row in blocks_of(where, False):
        outs[t][at : at + 8, :] = total[pl.ds(row, 8), :]


VMEM = pl.BlockSpec(memory_space=pltpu.VMEM)


def call_kernel(body, where, ins, a, rest, outs, block, scratch=(), in_any=0):
    rank = 32 * NX * NC
    cost = pl.CostEstimate(
        flops=12 * block[0] * block[1] * rank, bytes_accessed=4 * block[0] * block[1], transcendentals=0
    )
    return pl.pallas_call(
        body,
        in_specs=[pl.BlockSpec(memory_space=pltpu.SMEM)]
        + [VMEM] * (len(ins) - in_any)
        + [pl.BlockSpec()] * in_any
        + [pl.BlockSpec(memory_space=pltpu.HBM)]
        + [VMEM] * len(rest),
        out_specs=[VMEM] * len(outs),
        out_shape=outs,
        scratch_shapes=[
            pltpu.VMEM(block, jnp.float32),
            pltpu.SemaphoreType.DMA((block[0] // TILE,)),
            *scratch,
        ],
        cost_estimate=cost,
        compiler_params=pltpu.CompilerParams(vmem_limit_bytes=26 << 20),
    )(where, *ins, a, *rest)


def per_device(abundance, loadings, activity):
    f32, bf16 = jnp.float32, jnp.bfloat16
    rows, samples = abundance.shape
    own_rank, own_rows = loadings.shape[1], activity.shape[0]
    rank = own_rank * NX * NC
    half = rank // 2
    chunk = rows // CHUNKS
    kmer, samp = lax.axis_index("kmer"), lax.axis_index("samp")
    c = samp & 1
    where = jnp.stack([kmer >> 2, kmer & 3, samp >> 1, c, 1 - 2 * c]).astype(jnp.int32)
    shape = jax.ShapeDtypeStruct

    abundance = pltpu.with_memory_space_constraint(abundance, pltpu.HBM)
    w_mine = loadings.T
    h_parts = gather_ring4(gather_z(activity), "dy")
    w_own = jnp.concatenate(gather_ring4(w_mine, "dx"), axis=0)
    w_other = swap_cores(w_own)

    hh = hl = totals = None
    news = []
    for at in range(CHUNKS):
        wide = chunk + (LANES if at == 0 else 0)
        outs = [shape((own_rank, wide), f32)] * 4 + [shape((half, wide), f32)]
        block = (chunk, samples)
        if at == 0:
            *keep, send, hh, hl = call_kernel(
                first_rows_kernel,
                where,
                (w_own, w_other, *h_parts),
                abundance,
                (),
                outs + [shape((rank, samples), bf16)] * 2,
                block,
                [pltpu.VMEM((rank, samples), f32)],
                len(h_parts),
            )
        else:
            body = functools.partial(rows_kernel, at * chunk)
            ins = (w_own, w_other, hh, hl)
            *keep, send = call_kernel(body, where, ins, abundance, (), outs, block)
        got = swap_cores(send)
        parts = [k + got[own_rank * t : own_rank * (t + 1)] for t, k in enumerate(keep)]
        numer_w = scatter_ring4(parts, "dx")
        if at == 0:
            totals = numer_w[:, chunk : chunk + 1]
        mine, share = w_mine[:, at * chunk : (at + 1) * chunk], totals
        if news:
            mine, share, _ = lax.optimization_barrier((mine, share, news[-1]))
        news.append(mine * numer_w[:, :chunk] / share)

    hh, hl = (pltpu.with_memory_space_constraint(h, pltpu.HBM) for h in (hh, hl))
    pieces = []
    for at, new in enumerate(news):
        n_own = jnp.concatenate(gather_ring4(new, "dx"), axis=0)
        n_other = swap_cores(n_own)
        ins = (n_own, n_other, hh, hl)
        if at < CHUNKS - 1:
            (total,) = call_kernel(
                columns_kernel,
                where,
                ins,
                abundance,
                (),
                [shape((rank, samples + LANES), f32)],
                (chunk, samples),
                in_any=2,
            )
            continue
        width = samples // SPLIT
        for part in range(SPLIT):
            wide = width + (LANES if part == 0 else 0)
            body = functools.partial(last_columns_kernel, at * chunk, part * width)
            parts = call_kernel(
                body,
                where,
                ins,
                abundance,
                (total,),
                [shape((own_rows * NZ, wide), f32)] * 4,
                (chunk, width),
                [pltpu.VMEM((rank, wide), f32)],
                in_any=2,
            )
            pieces.append(scatter_ring4(parts, "dy"))
    first, *others = pieces
    joined = jnp.concatenate([first[:, :width], *others, first[:, width:]], axis=1)
    numer_h = scatter_z(joined)
    new_activity = activity * numer_h[:, :samples] / numer_h[:, samples : samples + 1]
    return (jnp.concatenate(news, axis=1).T, new_activity)


def solution(mesh):
    in_specs = (P("kmer", "samp"), P("kmer", "samp"), P("kmer", "samp"))
    out_specs = (P("kmer", "samp"), P("kmer", "samp"))
    return jax.shard_map(
        per_device, mesh=mesh, in_specs=in_specs, out_specs=out_specs, check_vma=False
    )
```
